1024 devices in a mesh: gx: 64 (over x, z), gy: 16 (over y, core).
Axes of the slice: x: 8, y: 8, z: 8, core: 2. Of those that a mesh axis runs over, the one named last changes fastest.
Arguments:
- blocks: float32 [64, 16, 64, 4, 128], P('gx', 'gy'), may hold values from 0 to 1, as said below
- active_counts: int32 [64, 16], P('gx', 'gy'), may hold values from 1 to 32, as said below
- pair_lists: int32 [64, 16, 32, 16], P('gx', 'gy'), may hold values from 0 to 575
- cell_ids: int32 [64, 16, 64], P('gx', 'gy'), may hold values from 0 to 511, as said below
Outputs:
- accel: float32 [64, 16, 32, 3, 128], P('gx', 'gy')
The draws below stay inside these ranges and needn't reach their ends.
Inputs may be any that keep to these rules, and one draw needn't show every extreme that they name: `active_counts`: every domain has at least one active block and some domain has 32; the active blocks are the first ones of the domain. `pair_lists`: entry (3 a + b) * 64 + n names block n of the domain a - 1 steps along gx and b - 1 steps along gy, with wrap around; a list may repeat a block or name the target block itself. `cell_ids`: A block of domain (i, j) lies in one of the 2 cells (g * 2 + h) with g = (i // 2) * (16 // 2) + j // 2. `blocks`: coordinates lie in [0, 1); masses are positive.
All inputs are finite; a program needn't handle non-finite values.
Results may differ from the reference program's by a relative error of at most 0.0003.
Values sent between devices are 32-bit elements; how exact they have to be, the bound alone decides.
A program may use at most 32 MiB of HBM per device.

```python
import jax
import jax.numpy as jnp
from jax import lax

BLOCK = 128
NB = 64
ACT = 32
KLIST = 16
SUBC = 2
N_GX = 64
N_GY = 16


def draw_blocks(key, part):
    key_pos = jax.random.fold_in(key, 11)
    key_mass = jax.random.fold_in(key, 12)
    shape_pos = (N_GX, N_GY, NB, 3, BLOCK)
    shape_mass = (N_GX, N_GY, NB, 1, BLOCK)
    position = jax.random.uniform(key_pos, shape_pos, jnp.float32)
    mass = jnp.exp(jax.random.uniform(key_mass, shape_mass, jnp.float32, jnp.log(0.5), jnp.log(2.0))) / (BLOCK * KLIST)
    return jnp.concatenate([position, mass], axis=3).astype(jnp.float32)


def draw_active_counts(key, part):
    counts = jax.random.randint(jax.random.fold_in(key, 21), (N_GX * N_GY,), 1, ACT + 1)
    where = jax.random.randint(jax.random.fold_in(key, 22), (), 0, N_GX * N_GY)
    counts = counts.at[where].set(ACT)
    return counts.reshape(N_GX, N_GY).astype(jnp.int32)


def draw_cell_ids(key, part):
    sub_cell = jax.random.randint(jax.random.fold_in(key, 31), (N_GX, N_GY, NB), 0, SUBC)
    row = jnp.arange(N_GX, dtype=jnp.int32)[:, None, None]
    col = jnp.arange(N_GY, dtype=jnp.int32)[None, :, None]
    group = row // 2 * (N_GY // 2) + col // 2
    return (group * SUBC + sub_cell).astype(jnp.int32)


def set_ends(entries, key, smallest, top_value):
    extent = entries.shape
    index_at = [jax.random.randint(jax.random.fold_in(key, axis), (), 0, extent[axis]) for axis in range(len(extent))]
    entries = entries.at[tuple(index_at)].set(smallest)
    longest = extent.index(max(extent))
    index_at[longest] = (index_at[longest] + 1) % extent[longest]
    return entries.at[tuple(index_at)].set(top_value)


def setup_inputs(seed: int = 0) -> dict:
    key_list = jax.random.split(jax.random.key(seed), 5)
    blocks = draw_blocks(jax.random.fold_in(key_list[4], 71), 0)
    active_counts = draw_active_counts(jax.random.fold_in(key_list[4], 71), 0)
    pair_lists = set_ends(jax.random.randint(key_list[2], (N_GX, N_GY, ACT, KLIST), 0, 9 * NB), jax.random.fold_in(key_list[2], 1), 0, (9 * NB) - 1).astype(jnp.int32)
    cell_ids = draw_cell_ids(jax.random.fold_in(key_list[4], 71), 0)
    return dict(blocks=blocks, active_counts=active_counts, pair_lists=pair_lists, cell_ids=cell_ids)


soft_near = 0.05
soft_far = 1.0


def pair_accel(target, sources):
    offset = sources[:, :3, None, :] - target[None, :3, :, None]
    dist_sq = jnp.sum(offset * offset, axis=1) + soft_near * soft_near
    weight = sources[:, 3, None, :] * dist_sq ** -1.5
    return jnp.sum(weight[:, None, :, :] * offset, axis=(0, 3))


def far_accel(position, centres, cell_mass):
    offset = centres[:, None, :] - position[:, :, None]
    dist_sq = jnp.sum(offset * offset, axis=0) + soft_far * soft_far
    weight = cell_mass[None, :] * dist_sq ** -1.5
    return jnp.sum(weight[None, :, :] * offset, axis=2)


def cell_centres(total, half_gy):
    cell = jnp.arange(total, dtype=jnp.int32)
    group = cell // SUBC
    sub_cell = cell % SUBC
    centre_x = (2 * (group // half_gy) + 1).astype(jnp.float32)
    centre_y = (2 * (group % half_gy) + 1).astype(jnp.float32)
    centre_z = (sub_cell.astype(jnp.float32) + 0.5) / SUBC
    return jnp.stack([centre_x, centre_y, centre_z], axis=0)


def reference(blocks, active_counts, pair_lists, cell_ids):
    total = (N_GX // 2) * (N_GY // 2) * SUBC
    block_mass = jnp.sum(blocks[:, :, :, 3, :], axis=-1)
    cell_mass = jax.ops.segment_sum(block_mass.reshape(-1), cell_ids.reshape(-1), num_segments=total)
    centres = cell_centres(total, N_GY // 2)

    def one_domain(device):
        row = device // N_GY
        col = device % N_GY
        pieces = []
        for step_a in range(3):
            for step_b in range(3):
                source = blocks[(row + step_a - 1) % N_GX, (col + step_b - 1) % N_GY]
                moved = jnp.array([step_a - 1, step_b - 1, 0, 0], dtype=jnp.float32)[:, None]
                pieces.append(source + moved)
        table = jnp.stack(pieces, axis=0).reshape(9 * NB, 4, BLOCK)
        local = blocks[row, col]
        corner = jnp.stack([row, col, 0]).astype(jnp.float32)[:, None]

        def one_slot(slot_index):
            target = local[slot_index]
            near = pair_accel(target, table[pair_lists[row, col, slot_index]])
            far = far_accel(target[:3] + corner, centres, cell_mass)
            return jnp.where(slot_index < active_counts[row, col], near + far, jnp.zeros_like(near))

        return lax.map(one_slot, jnp.arange(ACT, dtype=jnp.int32))

    result = lax.map(one_domain, jnp.arange(N_GX * N_GY, dtype=jnp.int32))
    return result.reshape(N_GX, N_GY, ACT, 3, BLOCK)
```

```python
import jax, jax.numpy as jnp
from jax import lax
from jax.experimental import pallas as pl
from jax.experimental.pallas import tpu as pltpu
from jax.sharding import PartitionSpec as P

EPS2 = 0.05 * 0.05

def split3(v):
    h = v.astype(jnp.bfloat16).astype(jnp.float32)
    r = v - h
    m = r.astype(jnp.bfloat16).astype(jnp.float32)
    return h, m, r - m

def compute_kernel(lists_ref, count_ref, tab_ref, mass_ref, out_ref, v_ref, p_ref, fb_ref, mb_ref):
    gx = lax.axis_index("gx").astype(jnp.float32)
    gy = lax.axis_index("gy").astype(jnp.float32)
    for q in range(9):
        a, b = q // 3 - 1, q % 3 - 1
        x = tab_ref[pl.ds(q * 256, 64, stride=4), :] + (a - 0.5)
        y = tab_ref[pl.ds(q * 256 + 1, 64, stride=4), :] + (b - 0.5)
        z = tab_ref[pl.ds(q * 256 + 2, 64, stride=4), :] - 0.5
        m = tab_ref[pl.ds(q * 256 + 3, 64, stride=4), :]
        s = x * x + y * y + z * z
        for k, val in enumerate((x, y, z, s, x, y, z, s)):
            v_ref[pl.ds(q * 512 + k, 64, stride=8), :] = val
        for k, val in enumerate((m, m * x, m * y, m * z)):
            p_ref[pl.ds(q * 256 + k, 64, stride=4), :] = val
    low = lax.broadcasted_iota(jnp.int32, (8, 128), 0) < 4
    ones = jnp.ones((8, 128), jnp.float32)

    def prep(i, c):
        for u in range(4):
            j = i * 4 + u
            h, m, l = split3(v_ref[pl.ds(j * 8, 8), :])
            f = jnp.concatenate([jnp.where(low, h, m), jnp.where(low, l, h), jnp.where(low, m, h), ones], axis=0)
            fb_ref[j] = f.astype(jnp.bfloat16)
        return c
    lax.fori_loop(0, 144, prep, 0)

    mt = jnp.transpose(mass_ref[...])
    mt = mt[:16, :]
    for g in range(32):
        mb_ref[g] = jnp.broadcast_to(mt[:, 2 * g:2 * g + 1] + mt[:, 2 * g + 1:2 * g + 2], (16, 128))

    row16 = lax.broadcasted_iota(jnp.int32, (16, 128), 0)
    cy = (2 * (row16 // 2) + 1).astype(jnp.float32) - gy
    cz = ((row16 % 2).astype(jnp.float32) + 0.5) * 0.5
    row8 = lax.broadcasted_iota(jnp.int32, (8, 128), 0)
    ws = (row8 & 3) == 3

    out_ref[...] = jnp.zeros_like(out_ref)

    def slot(t, c):
        base = 4 * 64 + t
        v = v_ref[pl.ds(base * 8, 8), :]
        q = v[3:4, :] + EPS2
        tv = -2.0 * v
        h, m, l = split3(tv)
        h = jnp.where(ws, 1.0, h)
        m = jnp.where(ws, 0.0, m)
        l = jnp.where(ws, 0.0, l)
        qh, qm, ql = split3(q)
        qg = jnp.where(row8 == 0, qh, jnp.where(row8 == 1, qm, jnp.where(row8 == 2, ql, 0.0)))
        tt = jnp.concatenate([h, jnp.where(low, h, m), jnp.where(low, m, l), qg], axis=0)
        tm = jnp.transpose(tt).astype(jnp.bfloat16)
        for k in range(8):
            i0, i1 = lists_ref[t, 2 * k], lists_ref[t, 2 * k + 1]
            f = jnp.concatenate([fb_ref[i0], fb_ref[i1]], axis=1)
            d = jnp.dot(tm, f, preferred_element_type=jnp.float32)
            r = lax.rsqrt(d)
            w = r * r * r
            for u, ii in enumerate((i0, i1)):
                wu = w[:, u * 128:(u + 1) * 128]
                g = [p_ref[pl.ds(ii * 4 + cc, 1), :] * wu for cc in range(4)]
                accs = g if (k == 0 and u == 0) else [x + y for x, y in zip(accs, g)]
        rr = [jnp.transpose(jnp.sum(x, axis=1, keepdims=True)) for x in accs]
        s0, sx, sy, sz = rr
        nx = sx - v[0:1, :] * s0
        ny = sy - v[1:2, :] * s0
        nz = sz - v[2:3, :] * s0
        px = v[0:1, :] + 0.5
        dy = cy - (v[1:2, :] + 0.5)
        dz = cz - (v[2:3, :] + 0.5)
        base2 = dy * dy + dz * dz + 1.0
        fb = jnp.zeros((16, 128), jnp.float32)
        fx = jnp.zeros((16, 128), jnp.float32)
        for g in range(32):
            dx = (2.0 * g + 1.0 - gx) - px
            r = lax.rsqrt(base2 + dx * dx)
            w = (r * r) * (r * mb_ref[g])
            fb = fb + w
            fx = fx + w * dx
        ax = jnp.sum(fx, axis=0, keepdims=True)
        ay = jnp.sum(fb * dy, axis=0, keepdims=True)
        az = jnp.sum(fb * dz, axis=0, keepdims=True)
        out_ref[t] = jnp.concatenate([nx + ax, ny + ay, nz + az], axis=0)
        return c
    lax.fori_loop(0, count_ref[0, 0], slot, 0)

def compute(tab, mass, lists, count):
    return pl.pallas_call(
        compute_kernel,
        out_shape=jax.ShapeDtypeStruct((32, 3, 128), jnp.float32),
        in_specs=[pl.BlockSpec(memory_space=pltpu.SMEM)] * 2 + [pl.BlockSpec(memory_space=pltpu.VMEM)] * 2,
        out_specs=pl.BlockSpec(memory_space=pltpu.VMEM),
        scratch_shapes=[pltpu.VMEM((4608, 128), jnp.float32), pltpu.VMEM((2304, 128), jnp.float32),
                        pltpu.VMEM((576, 32, 128), jnp.bfloat16),
                        pltpu.VMEM((32, 16, 128), jnp.float32)],
        name="near_far",
    )(lists, count, tab, mass)


NCH = 2
MESH = pl.DeviceIdType.MESH


def comm_kernel(ids_ref, blk_ref, mrow_ref, tab_ref, mx_ref, row1_ref, got1_ref, row2_ref, mz_ref,
                hs_sem, hr_sem, s1, r1, s2, r2, s3, r3, loc_sem):
    nx, ny = 64, 16
    gx, gy = lax.axis_index("gx"), lax.axis_index("gy")
    xi, zi = gx // 8, gx % 8
    xp, xm = lax.rem(gx + 1, nx), lax.rem(gx + nx - 1, nx)
    yp, ym = lax.rem(gy + 1, ny), lax.rem(gy + ny - 1, ny)

    def ypeer(d):
        return (gx, lax.rem(gy + d, ny))

    def zpeer(d):
        return (xi * 8 + lax.rem(zi + d, 8), gy)

    def xpeer(d):
        return (lax.rem(xi + d, 8) * 8 + zi, gy)

    barrier = pltpu.get_barrier_semaphore()
    for d in range(1, ny):
        pl.semaphore_signal(barrier, inc=1, device_id=ypeer(d), device_id_type=MESH)
    for d in range(1, 8):
        pl.semaphore_signal(barrier, inc=1, device_id=zpeer(d), device_id_type=MESH)
        pl.semaphore_signal(barrier, inc=1, device_id=xpeer(d), device_id_type=MESH)
    pl.semaphore_signal(barrier, inc=1, device_id=(xp, gy), device_id_type=MESH)
    pl.semaphore_signal(barrier, inc=1, device_id=(xm, gy), device_id_type=MESH)

    own = pltpu.make_async_copy(blk_ref, tab_ref.at[4], loc_sem)
    own.start()

    m = mrow_ref[...]
    ids = jnp.broadcast_to(ids_ref[...] % 2, (64, 64)).astype(jnp.float32)
    eye = lax.broadcasted_iota(jnp.int32, (64, 64), 0) == lax.broadcasted_iota(jnp.int32, (64, 64), 1)
    half = jnp.sum(jnp.where(eye, ids, 0.0), axis=1, keepdims=True)
    upper = jnp.sum(jnp.sum(jnp.where(half > 0.5, m, 0.0), axis=0, keepdims=True), axis=1, keepdims=True)
    lower = jnp.sum(jnp.sum(jnp.where(half > 0.5, 0.0, m), axis=0, keepdims=True), axis=1, keepdims=True)
    lane = lax.broadcasted_iota(jnp.int32, (1, 128), 1)
    at = (gy // 2) * 2
    row = jnp.where(lane == at, lower, jnp.where(lane == at + 1, upper, 0.0))
    row1_ref[...] = row

    pl.semaphore_wait(barrier, 31)

    phase1 = [
        pltpu.make_async_remote_copy(row1_ref, got1_ref.at[d - 1], s1.at[d - 1], r1.at[d - 1],
                                     device_id=ypeer(d), device_id_type=MESH)
        for d in range(1, ny)
    ]
    for c in phase1:
        c.start()

    size = 64 // NCH

    def halo(index, ch, source, slot, device):
        part = pl.ds(ch * size, size)
        src = blk_ref.at[part] if source is None else tab_ref.at[source, part]
        k = index * NCH + ch
        return pltpu.make_async_remote_copy(src, tab_ref.at[slot, part], hs_sem.at[k], hr_sem.at[k],
                                            device_id=device, device_id_type=MESH)

    toxp = [halo(0, ch, None, 1, (xp, gy)) for ch in range(NCH)]
    toxm = [halo(1, ch, None, 7, (xm, gy)) for ch in range(NCH)]
    toyp = [halo(2, ch, None, 3, (gx, yp)) for ch in range(NCH)]
    toym = [halo(3, ch, None, 5, (gx, ym)) for ch in range(NCH)]
    fwd = []
    for ch in range(NCH):
        for c in (toxp, toxm, toyp, toym):
            c[ch].start()

    for c in phase1:
        c.wait_recv()
    total = row
    for d in range(1, ny):
        total = total + got1_ref[d - 1]
    row2_ref[...] = total
    mz_ref[zi] = total

    def forward(ch):
        toxp[ch].wait_recv()
        toxm[ch].wait_recv()
        for index, source, slot, device in ((4, 1, 0, (gx, yp)), (5, 7, 6, (gx, yp)),
                                            (6, 1, 2, (gx, ym)), (7, 7, 8, (gx, ym))):
            c = halo(index, ch, source, slot, device)
            c.start()
            fwd.append(c)

    phase2 = [
        pltpu.make_async_remote_copy(row2_ref, mz_ref.at[zi], s2.at[d - 1], r2.at[d - 1],
                                     device_id=zpeer(d), device_id_type=MESH)
        for d in range(1, 8)
    ]
    for c in phase2:
        c.start()
    forward(0)
    for d in range(1, 8):
        phase2[d - 1].wait_recv()
    phase3 = [
        pltpu.make_async_remote_copy(mz_ref, mx_ref.at[xi], s3.at[d - 1], r3.at[d - 1],
                                     device_id=xpeer(d), device_id_type=MESH)
        for d in range(1, 8)
    ]
    for c in phase3:
        c.start()
    mx_ref[xi] = mz_ref[...]
    for ch in range(1, NCH):
        forward(ch)
    for c in toyp + toym:
        c.wait_recv()
    for c in fwd:
        c.wait_recv()
    for c in phase3:
        c.wait_recv()
    for c in phase1 + phase2 + phase3 + toxp + toxm + toyp + toym + fwd:
        c.wait_send()
    own.wait()


def exchange(ids, blk, mrow):
    return pl.pallas_call(
        comm_kernel,
        out_shape=(jax.ShapeDtypeStruct((9, 64, 4, 128), jnp.float32),
                   jax.ShapeDtypeStruct((8, 8, 1, 128), jnp.float32)),
        in_specs=[pl.BlockSpec(memory_space=pltpu.VMEM), pl.BlockSpec(memory_space=pl.ANY),
                  pl.BlockSpec(memory_space=pltpu.VMEM)],
        out_specs=(pl.BlockSpec(memory_space=pl.ANY), pl.BlockSpec(memory_space=pltpu.VMEM)),
        scratch_shapes=[
            pltpu.VMEM((1, 128), jnp.float32),
            pltpu.VMEM((15, 1, 128), jnp.float32),
            pltpu.VMEM((1, 128), jnp.float32),
            pltpu.VMEM((8, 1, 128), jnp.float32),
            pltpu.SemaphoreType.DMA((8 * NCH,)), pltpu.SemaphoreType.DMA((8 * NCH,)),
            pltpu.SemaphoreType.DMA((15,)), pltpu.SemaphoreType.DMA((15,)),
            pltpu.SemaphoreType.DMA((7,)), pltpu.SemaphoreType.DMA((7,)),
            pltpu.SemaphoreType.DMA((7,)), pltpu.SemaphoreType.DMA((7,)),
            pltpu.SemaphoreType.DMA,
        ],
        compiler_params=pltpu.CompilerParams(collective_id=0, has_side_effects=True),
        name="exchange",
    )(ids, blk, mrow)


def body(blocks, active_counts, pair_lists, cell_ids):
    blk = blocks[0, 0]
    tab, mass = exchange(cell_ids[0], blk, blk[:, 3, :])
    out = compute(tab.reshape(2304, 128), mass.reshape(64, 128), pair_lists[0, 0], active_counts)
    return out[None, None]


def solution(mesh):
    in_specs = (P("gx", "gy", None, None, None), P("gx", "gy"), P("gx", "gy", None, None), P("gx", "gy", None))
    return jax.shard_map(body, mesh=mesh, in_specs=in_specs, out_specs=P("gx", "gy", None, None, None),
                         check_vma=False)
```

```python
import jax
import jax.numpy as jnp
from jax import lax
from jax.experimental import pallas as pl
from jax.experimental.pallas import tpu as pltpu
from jax.sharding import PartitionSpec as P

MESH = pl.DeviceIdType.MESH
EPS2 = 0.05 * 0.05
NCH = 2
UN = 2
MX = (0, 2, 4, 6)
DN = (((1,), (1,)), ((), ()))


def split3(v):
    h = v.astype(jnp.bfloat16).astype(jnp.float32)
    r = v - h
    m = r.astype(jnp.bfloat16).astype(jnp.float32)
    return h, m, r - m


def near_kernel(lists_ref, ids_ref, blk_ref, near_ref, mx_ref, tab_ref, v_ref, p_ref, fb_ref, pb_ref, tm_ref, red_ref,
                red2_ref, row1_ref, got1_ref, row2_ref, mz_ref, hs_sem, hr_sem, s1, r1, s2, r2, s3, r3, loc_sem):
    nx, ny = 64, 16
    gx, gy = lax.axis_index("gx"), lax.axis_index("gy")
    xi, zi = gx // 8, gx % 8
    xp, xm = lax.rem(gx + 1, nx), lax.rem(gx + nx - 1, nx)
    yp, ym = lax.rem(gy + 1, ny), lax.rem(gy + ny - 1, ny)

    def ypeer(d):
        return (gx, lax.rem(gy + d, ny))

    def zpeer(d):
        return (xi * 8 + lax.rem(zi + d, 8), gy)

    def xpeer(d):
        return (lax.rem(xi + d, 8) * 8 + zi, gy)

    barrier = pltpu.get_barrier_semaphore()
    for d in range(1, ny):
        pl.semaphore_signal(barrier, inc=1, device_id=ypeer(d), device_id_type=MESH)
    for d in range(1, 8):
        pl.semaphore_signal(barrier, inc=1, device_id=zpeer(d), device_id_type=MESH)
        pl.semaphore_signal(barrier, inc=1, device_id=xpeer(d), device_id_type=MESH)
    pl.semaphore_signal(barrier, inc=1, device_id=(xp, gy), device_id_type=MESH)
    pl.semaphore_signal(barrier, inc=1, device_id=(xm, gy), device_id_type=MESH)

    own = pltpu.make_async_copy(blk_ref, tab_ref.at[pl.ds(1024, 256)], loc_sem)
    own.start()
    own.wait()

    m = tab_ref[pl.ds(1024 + 3, 64, stride=4), :]
    ids = jnp.broadcast_to(ids_ref[...] % 2, (64, 64)).astype(jnp.float32)
    eye = lax.broadcasted_iota(jnp.int32, (64, 64), 0) == lax.broadcasted_iota(jnp.int32, (64, 64), 1)
    half = jnp.sum(jnp.where(eye, ids, 0.0), axis=1, keepdims=True)
    upper = jnp.sum(jnp.sum(jnp.where(half > 0.5, m, 0.0), axis=0, keepdims=True), axis=1, keepdims=True)
    lower = jnp.sum(jnp.sum(jnp.where(half > 0.5, 0.0, m), axis=0, keepdims=True), axis=1, keepdims=True)
    lane = lax.broadcasted_iota(jnp.int32, (1, 128), 1)
    at = (gy // 2) * 2
    row = jnp.where(lane == at, lower, jnp.where(lane == at + 1, upper, 0.0))
    row1_ref[...] = row

    low = lax.broadcasted_iota(jnp.int32, (8, 128), 0) < 4
    ones = jnp.ones((8, 128), jnp.float32)

    def prepare(q):
        a, b = q // 3 - 1, q % 3 - 1
        x = tab_ref[pl.ds(q * 256, 64, stride=4), :] + (a - 0.5)
        y = tab_ref[pl.ds(q * 256 + 1, 64, stride=4), :] + (b - 0.5)
        z = tab_ref[pl.ds(q * 256 + 2, 64, stride=4), :] - 0.5
        m = tab_ref[pl.ds(q * 256 + 3, 64, stride=4), :]
        s = x * x + y * y + z * z
        for k, val in enumerate((x, y, z, s, x, y, z, s)):
            v_ref[pl.ds(q * 512 + k, 64, stride=8), :] = val
        for k, val in enumerate((m, m * x, m * y, m * z)):
            p_ref[pl.ds(q * 256 + k, 64, stride=4), :] = val

        def step(i, c):
            for u in range(4):
                j = q * 64 + i * 4 + u
                h, m, l = split3(v_ref[pl.ds(j * 8, 8), :])
                f = jnp.concatenate([jnp.where(low, h, m), jnp.where(low, l, h), jnp.where(low, m, h), ones], axis=0)
                fb_ref[j] = f.astype(jnp.bfloat16)
                h, m, l = split3(p_ref[pl.ds(j * 4, 4), :])
                pb_ref[j] = jnp.concatenate([h, m, l, l], axis=0).astype(jnp.bfloat16)
            return c

        lax.fori_loop(0, 16, step, 0)

    prepare(4)

    row8 = lax.broadcasted_iota(jnp.int32, (8, 128), 0)
    ws = (row8 & 3) == 3

    def targets(i, c):
        for u in range(4):
            t = i * 4 + u
            v = v_ref[pl.ds((256 + t) * 8, 8), :]
            h, m, l = split3(-2.0 * v)
            h = jnp.where(ws, 1.0, h)
            m = jnp.where(ws, 0.0, m)
            l = jnp.where(ws, 0.0, l)
            qh, qm, ql = split3(v[3:4, :] + EPS2)
            qg = jnp.where(row8 == 0, qh, jnp.where(row8 == 1, qm, jnp.where(row8 == 2, ql, 0.0)))
            tt = jnp.concatenate([h, jnp.where(low, h, m), jnp.where(low, m, l), qg], axis=0)
            tm_ref[t] = jnp.transpose(tt).astype(jnp.bfloat16)
        return c

    lax.fori_loop(0, 8, targets, 0)
    red_ref[0:UN] = jnp.zeros((UN, 128, 128), jnp.float32)
    red2_ref[0:UN] = jnp.zeros((UN, 128, 16), jnp.float32)

    pl.semaphore_wait(barrier, 31)

    phase1 = [
        pltpu.make_async_remote_copy(row1_ref, got1_ref.at[d - 1], s1.at[d - 1], r1.at[d - 1],
                                     device_id=ypeer(d), device_id_type=MESH)
        for d in range(1, ny)
    ]
    for c in phase1:
        c.start()

    size = 256 // NCH

    def halo(index, ch, source, slot, device):
        src = blk_ref.at[pl.ds(ch * size, size)] if source is None else tab_ref.at[pl.ds(source * 256 + ch * size, size)]
        k = index * NCH + ch
        return pltpu.make_async_remote_copy(src, tab_ref.at[pl.ds(slot * 256 + ch * size, size)], hs_sem.at[k],
                                            hr_sem.at[k], device_id=device, device_id_type=MESH)

    toxp = [halo(0, ch, None, 1, (xp, gy)) for ch in range(NCH)]
    toxm = [halo(1, ch, None, 7, (xm, gy)) for ch in range(NCH)]
    toyp = [halo(2, ch, None, 3, (gx, yp)) for ch in range(NCH)]
    toym = [halo(3, ch, None, 5, (gx, ym)) for ch in range(NCH)]
    fwd = {4: [], 5: [], 6: [], 7: []}
    for ch in range(NCH):
        for c in (toxp, toxm, toyp, toym):
            c[ch].start()

    def forward(ch):
        for index, arrived, source, slot, device in ((4, toxp, 1, 0, (gx, yp)), (6, None, 1, 2, (gx, ym)),
                                                     (5, toxm, 7, 6, (gx, yp)), (7, None, 7, 8, (gx, ym))):
            if arrived is not None:
                arrived[ch].wait_recv()
            c = halo(index, ch, source, slot, device)
            c.start()
            fwd[index].append(c)

    forward(0)
    for c in phase1:
        c.wait_recv()
    total = row
    for d in range(1, ny):
        total = total + got1_ref[d - 1]
    row2_ref[...] = total
    mz_ref[zi] = total
    for ch in range(1, NCH):
        forward(ch)
    phase2 = [
        pltpu.make_async_remote_copy(row2_ref, mz_ref.at[zi], s2.at[d - 1], r2.at[d - 1],
                                     device_id=zpeer(d), device_id_type=MESH)
        for d in range(1, 8)
    ]
    for c in phase2:
        c.start()
    prepare(1)
    prepare(7)
    for c in toyp:
        c.wait_recv()
    prepare(3)
    for c in toym:
        c.wait_recv()
    prepare(5)
    for index, slot in ((4, 0), (6, 2), (5, 6), (7, 8)):
        for c in fwd[index]:
            c.wait_recv()
        prepare(slot)
    for c in phase2:
        c.wait_recv()
    phase3 = [
        pltpu.make_async_remote_copy(mz_ref, mx_ref.at[xi], s3.at[d - 1], r3.at[d - 1],
                                     device_id=xpeer(d), device_id_type=MESH)
        for d in range(1, 8)
    ]
    for c in phase3:
        c.start()
    mx_ref[xi] = mz_ref[...]

    lane128 = lax.broadcasted_iota(jnp.int32, (128, 128), 1)

    def pairs(t):
        tm = tm_ref[t]
        accs, acc2 = None, None
        for k in range(8):
            i0, i1 = lists_ref[2 * k, t], lists_ref[2 * k + 1, t]
            f = jnp.concatenate([fb_ref[i0], fb_ref[i1]], axis=1)
            d = jnp.dot(tm, f, preferred_element_type=jnp.float32)
            r = lax.rsqrt(d)
            w = r * r * r
            if k in MX:
                p = jnp.concatenate([pb_ref[i0], pb_ref[i1]], axis=1)
                hi = w.astype(jnp.bfloat16)
                lo = (w - hi.astype(jnp.float32)).astype(jnp.bfloat16)
                y = lax.dot_general(hi, p, DN, preferred_element_type=jnp.float32)
                acc2 = y if acc2 is None else acc2 + y
                acc2 = acc2 + lax.dot_general(lo, p, DN, preferred_element_type=jnp.float32)
                continue
            for u, ii in enumerate((i0, i1)):
                wu = w[:, u * 128:(u + 1) * 128]
                g = [p_ref[pl.ds(ii * 4 + cc, 1), :] * wu for cc in range(4)]
                accs = g if accs is None else [x + y for x, y in zip(accs, g)]
        red2_ref[t] = acc2
        rr = [jnp.sum(x, axis=1, keepdims=True) for x in accs]
        red_ref[t] = jnp.where(lane128 == 0, rr[0], jnp.where(lane128 == 1, rr[1], jnp.where(lane128 == 2, rr[2], rr[3])))

    def reduce(t):
        v = v_ref[pl.ds((256 + t) * 8, 8), :]
        r2 = jnp.transpose(red2_ref[t])
        red = jnp.transpose(red_ref[t])[0:4] + (r2[0:4] + r2[4:8] + r2[8:12])
        for c in range(3):
            near_ref[c, pl.ds(t, 1), :] = red[c + 1:c + 2] - v[c:c + 1, :] * red[0:1]

    def slots(i, c):
        for u in range(UN):
            pairs(i * UN + u)
        for u in range(UN):
            reduce(jnp.maximum(i - 1, 0) * UN + u)
        return c

    lax.fori_loop(0, 32 // UN, slots, 0)
    for u in range(UN):
        reduce(32 - UN + u)

    for c in phase3:
        c.wait_recv()
    for c in phase1 + phase2 + phase3 + toxp + toxm + toyp + toym + fwd[4] + fwd[5] + fwd[6] + fwd[7]:
        c.wait_send()


def near(lists, ids, blk):
    dma = pltpu.SemaphoreType.DMA
    return pl.pallas_call(
        near_kernel,
        out_shape=(jax.ShapeDtypeStruct((3, 32, 128), jnp.float32), jax.ShapeDtypeStruct((8, 8, 1, 128), jnp.float32)),
        in_specs=[pl.BlockSpec(memory_space=pltpu.SMEM), pl.BlockSpec(memory_space=pltpu.VMEM),
                  pl.BlockSpec(memory_space=pl.ANY)],
        out_specs=(pl.BlockSpec(memory_space=pltpu.VMEM), pl.BlockSpec(memory_space=pltpu.VMEM)),
        scratch_shapes=[
            pltpu.VMEM((2304, 128), jnp.float32), pltpu.VMEM((4608, 128), jnp.float32),
            pltpu.VMEM((2304, 128), jnp.float32), pltpu.VMEM((576, 32, 128), jnp.bfloat16),
            pltpu.VMEM((576, 16, 128), jnp.bfloat16), pltpu.VMEM((32, 128, 32), jnp.bfloat16),
            pltpu.VMEM((32, 128, 128), jnp.float32), pltpu.VMEM((32, 128, 16), jnp.float32),
            pltpu.VMEM((1, 128), jnp.float32), pltpu.VMEM((15, 1, 128), jnp.float32),
            pltpu.VMEM((1, 128), jnp.float32), pltpu.VMEM((8, 1, 128), jnp.float32),
            dma((8 * NCH,)), dma((8 * NCH,)), dma((15,)), dma((15,)), dma((7,)), dma((7,)), dma((7,)), dma((7,)), dma,
        ],
        compiler_params=pltpu.CompilerParams(collective_id=0, has_side_effects=True),
        name="near",
    )(lists, ids, blk)


def far_kernel(count_ref, blk_ref, mass_ref, near_ref, out_ref, mb_ref):
    gx = lax.axis_index("gx").astype(jnp.float32)
    gy = lax.axis_index("gy").astype(jnp.float32)
    mt = jnp.transpose(mass_ref[...])[:16, :]
    for g in range(32):
        mb_ref[pl.ds(g * 16, 16), :] = jnp.broadcast_to(mt[:, 2 * g:2 * g + 1] + mt[:, 2 * g + 1:2 * g + 2], (16, 128))
    row8 = lax.broadcasted_iota(jnp.int32, (8, 128), 0)

    def group(s, c):
        x = blk_ref[pl.ds(s * 32, 8, stride=4), :]
        y = blk_ref[pl.ds(s * 32 + 1, 8, stride=4), :]
        z = blk_ref[pl.ds(s * 32 + 2, 8, stride=4), :]
        dz = [0.25 - z, 0.75 - z]
        dy = [(2.0 * j + 1.0 - gy) - y for j in range(8)]
        zz = [d * d + 1.0 for d in dz]
        yy = [d * d for d in dy]
        base = [[yy[j] + zz[h] for h in range(2)] for j in range(8)]
        by, bz, ax = [None] * 8, [None] * 2, None
        for g in range(32):
            dx = (2.0 * g + 1.0 - gx) - x
            xx = dx * dx
            total = None
            for j in range(8):
                w = []
                for h in range(2):
                    r = lax.rsqrt(base[j][h] + xx)
                    v = (r * r) * (r * mb_ref[pl.ds(g * 16 + j * 2 + h, 1), :])
                    w.append(v)
                bz[1] = w[1] if bz[1] is None else bz[1] + w[1]
                bz[0] = w[0] if bz[0] is None else bz[0] + w[0]
                both = w[0] + w[1]
                by[j] = both if by[j] is None else by[j] + both
                total = both if total is None else total + both
            ax = total * dx if ax is None else ax + total * dx
        ay = by[0] * dy[0]
        for j in range(1, 8):
            ay = ay + by[j] * dy[j]
        az = bz[0] * dz[0] + bz[1] * dz[1]
        active = row8 + s * 8 < count_ref[0, 0]
        for k, val in enumerate((ax, ay, az)):
            at = pl.ds(pl.multiple_of(s * 8, 8), 8)
            out_ref[k, at, :] = jnp.where(active, near_ref[k, at, :] + val, 0.0)
        return c

    lax.fori_loop(0, 4, group, 0)


def far(count, blk, mass, near_part):
    return pl.pallas_call(
        far_kernel,
        out_shape=jax.ShapeDtypeStruct((3, 32, 128), jnp.float32),
        in_specs=[pl.BlockSpec(memory_space=pltpu.SMEM)] + [pl.BlockSpec(memory_space=pltpu.VMEM)] * 3,
        out_specs=pl.BlockSpec(memory_space=pltpu.VMEM),
        scratch_shapes=[pltpu.VMEM((512, 128), jnp.float32)],
        name="far",
    )(count, blk, mass, near_part)


def body(blocks, active_counts, pair_lists, cell_ids):
    blk = blocks.reshape(256, 128)
    near_part, mass = near(pair_lists[0, 0].T, cell_ids[0], blk)
    out = far(active_counts, blk, mass.reshape(64, 128), near_part)
    return out.transpose(1, 0, 2)[None, None]


def solution(mesh):
    in_specs = (P("gx", "gy", None, None, None), P("gx", "gy"), P("gx", "gy", None, None), P("gx", "gy", None))
    return jax.shard_map(body, mesh=mesh, in_specs=in_specs, out_specs=P("gx", "gy", None, None, None),
                         check_vma=False)
```

```python
import jax
import jax.numpy as jnp
from jax import lax
from jax.experimental import pallas as pl
from jax.experimental.pallas import tpu as pltpu
from jax.sharding import PartitionSpec as P

MESH = pl.DeviceIdType.MESH
EPS2 = 0.05 * 0.05
NCH = 4
UN = 4
MX = (0, 2, 4, 6)
DN = (((1,), (1,)), ((), ()))


def split3(v):
    h = v.astype(jnp.bfloat16).astype(jnp.float32)
    r = v - h
    m = r.astype(jnp.bfloat16).astype(jnp.float32)
    return h, m, r - m


def force_kernel(lists_ref, count_ref, ids_ref, blk_ref, out_ref, mx_ref, near_ref, q_ref, mb_ref, tab_ref, v_ref, p_ref, fb_ref, pb_ref, tm_ref, red_ref,
                red2_ref, row1_ref, got1_ref, row2_ref, mz_ref, hs_sem, hr_sem, s1, r1, s2, r2, s3, r3, loc_sem):
    nx, ny = 64, 16
    gx, gy = lax.axis_index("gx"), lax.axis_index("gy")
    xi, zi = gx // 8, gx % 8
    xp, xm = lax.rem(gx + 1, nx), lax.rem(gx + nx - 1, nx)
    yp, ym = lax.rem(gy + 1, ny), lax.rem(gy + ny - 1, ny)

    def ypeer(d):
        return (gx, lax.rem(gy + d, ny))

    def zpeer(d):
        return (xi * 8 + lax.rem(zi + d, 8), gy)

    def xpeer(d):
        return (lax.rem(xi + d, 8) * 8 + zi, gy)

    barrier = pltpu.get_barrier_semaphore()
    for d in range(1, ny):
        pl.semaphore_signal(barrier, inc=1, device_id=ypeer(d), device_id_type=MESH)
    for d in range(1, 8):
        pl.semaphore_signal(barrier, inc=1, device_id=zpeer(d), device_id_type=MESH)
        pl.semaphore_signal(barrier, inc=1, device_id=xpeer(d), device_id_type=MESH)
    pl.semaphore_signal(barrier, inc=1, device_id=(xp, gy), device_id_type=MESH)
    pl.semaphore_signal(barrier, inc=1, device_id=(xm, gy), device_id_type=MESH)

    own = pltpu.make_async_copy(blk_ref, tab_ref.at[pl.ds(1024, 256)], loc_sem)
    own.start()

    pl.semaphore_wait(barrier, 31)

    size = 256 // NCH

    def halo(index, ch, source, slot, device):
        src = blk_ref.at[pl.ds(ch * size, size)] if source is None else tab_ref.at[pl.ds(source * 256 + ch * size, size)]
        k = index * NCH + ch
        return pltpu.make_async_remote_copy(src, tab_ref.at[pl.ds(slot * 256 + ch * size, size)], hs_sem.at[k],
                                            hr_sem.at[k], device_id=device, device_id_type=MESH)

    toxp = [halo(0, ch, None, 1, (xp, gy)) for ch in range(NCH)]
    toxm = [halo(1, ch, None, 7, (xm, gy)) for ch in range(NCH)]
    toyp = [halo(2, ch, None, 3, (gx, yp)) for ch in range(NCH)]
    toym = [halo(3, ch, None, 5, (gx, ym)) for ch in range(NCH)]
    fwd = {4: [], 5: [], 6: [], 7: []}
    for ch in range(NCH):
        for c in (toxp, toxm, toyp, toym):
            c[ch].start()

    own.wait()

    m = tab_ref[pl.ds(1024 + 3, 64, stride=4), :]
    ids = jnp.broadcast_to(ids_ref[...] % 2, (64, 64)).astype(jnp.float32)
    eye = lax.broadcasted_iota(jnp.int32, (64, 64), 0) == lax.broadcasted_iota(jnp.int32, (64, 64), 1)
    half = jnp.sum(jnp.where(eye, ids, 0.0), axis=1, keepdims=True)
    upper = jnp.sum(jnp.sum(jnp.where(half > 0.5, m, 0.0), axis=0, keepdims=True), axis=1, keepdims=True)
    lower = jnp.sum(jnp.sum(jnp.where(half > 0.5, 0.0, m), axis=0, keepdims=True), axis=1, keepdims=True)
    lane = lax.broadcasted_iota(jnp.int32, (1, 128), 1)
    at = (gy // 2) * 2
    row = jnp.where(lane == at, lower, jnp.where(lane == at + 1, upper, 0.0))
    row1_ref[...] = row

    phase1 = [
        pltpu.make_async_remote_copy(row1_ref, got1_ref.at[d - 1], s1.at[d - 1], r1.at[d - 1],
                                     device_id=ypeer(d), device_id_type=MESH)
        for d in range(1, ny)
    ]
    for c in phase1:
        c.start()

    low = lax.broadcasted_iota(jnp.int32, (8, 128), 0) < 4
    ones = jnp.ones((8, 128), jnp.float32)

    def prepare(q):
        a, b = q // 3 - 1, q % 3 - 1
        x = tab_ref[pl.ds(q * 256, 64, stride=4), :] + (a - 0.5)
        y = tab_ref[pl.ds(q * 256 + 1, 64, stride=4), :] + (b - 0.5)
        z = tab_ref[pl.ds(q * 256 + 2, 64, stride=4), :] - 0.5
        m = tab_ref[pl.ds(q * 256 + 3, 64, stride=4), :]
        s = x * x + y * y + z * z
        for k, val in enumerate((x, y, z, s, x, y, z, s)):
            v_ref[pl.ds(q * 512 + k, 64, stride=8), :] = val
        for k, val in enumerate((m, m * x, m * y, m * z) * 2):
            p_ref[pl.ds(q * 512 + k, 64, stride=8), :] = val

        def step(i, c):
            for u in range(4):
                j = q * 64 + i * 4 + u
                h, m, l = split3(v_ref[pl.ds(j * 8, 8), :])
                f = jnp.concatenate([jnp.where(low, h, m), jnp.where(low, l, h), jnp.where(low, m, h), ones], axis=0)
                fb_ref[j] = f.astype(jnp.bfloat16)
                h, m, l = split3(p_ref[pl.ds(j * 8, 8), :])
                pb_ref[j] = jnp.concatenate([jnp.where(low, h, m), l], axis=0).astype(jnp.bfloat16)
            return c

        lax.fori_loop(0, 16, step, 0)

    row8 = lax.broadcasted_iota(jnp.int32, (8, 128), 0)
    ws = (row8 & 3) == 3

    def targets(i, c):
        for u in range(4):
            t = i * 4 + u
            v = v_ref[pl.ds((256 + t) * 8, 8), :]
            h, m, l = split3(-2.0 * v)
            h = jnp.where(ws, 1.0, h)
            m = jnp.where(ws, 0.0, m)
            l = jnp.where(ws, 0.0, l)
            qh, qm, ql = split3(v[3:4, :] + EPS2)
            qg = jnp.where(row8 == 0, qh, jnp.where(row8 == 1, qm, jnp.where(row8 == 2, ql, 0.0)))
            tt = jnp.concatenate([h, jnp.where(low, h, m), jnp.where(low, m, l), qg], axis=0)
            tm_ref[t] = jnp.transpose(tt).astype(jnp.bfloat16)
        return c

    def forward(ch):
        for index, arrived, source, slot, device in ((4, toxp, 1, 0, (gx, yp)), (6, None, 1, 2, (gx, ym)),
                                                     (5, toxm, 7, 6, (gx, yp)), (7, None, 7, 8, (gx, ym))):
            if arrived is not None:
                arrived[ch].wait_recv()
            c = halo(index, ch, source, slot, device)
            c.start()
            fwd[index].append(c)

    fgx, fgy = gx.astype(jnp.float32), gy.astype(jnp.float32)

    def offsets(s):
        x = tab_ref[pl.ds(1024 + s * 32, 8, stride=4), :]
        y = tab_ref[pl.ds(1024 + s * 32 + 1, 8, stride=4), :]
        z = tab_ref[pl.ds(1024 + s * 32 + 2, 8, stride=4), :]
        return x, [(2.0 * j + 1.0 - fgy) - y for j in range(8)], [0.25 - z, 0.75 - z]

    def weights(s):
        x, dy, dz = offsets(s)
        zz = [d * d + 1.0 for d in dz]
        yy = [d * d for d in dy]
        base = [yy[j] + zz[h] for j in range(8) for h in range(2)]

        def step(i, c):
            for u in range(4):
                g = i * 4 + u
                dx = (2.0 * g.astype(jnp.float32) + 1.0 - fgx) - x
                xx = dx * dx
                for k in range(16):
                    r = lax.rsqrt(base[k] + xx)
                    q_ref[s, g * 16 + k] = r * r * r
            return c

        lax.fori_loop(0, 8, step, 0)

    prepare(4)
    for ch in range(NCH):
        forward(ch)
        weights(ch)
    lax.fori_loop(0, 8, targets, 0)
    red_ref[0:UN] = jnp.zeros((UN, 128, 128), jnp.float32)
    red2_ref[0:UN] = jnp.zeros((UN, 128, 16), jnp.float32)
    for c in phase1:
        c.wait_recv()
    total = row
    for d in range(1, ny):
        total = total + got1_ref[d - 1]
    row2_ref[...] = total
    mz_ref[zi] = total
    phase2 = [
        pltpu.make_async_remote_copy(row2_ref, mz_ref.at[zi], s2.at[d - 1], r2.at[d - 1],
                                     device_id=zpeer(d), device_id_type=MESH)
        for d in range(1, 8)
    ]
    for c in phase2:
        c.start()
    prepare(1)
    prepare(7)
    for c in toyp:
        c.wait_recv()
    prepare(3)
    for c in toym:
        c.wait_recv()
    prepare(5)
    for index, slot in ((4, 0), (6, 2), (5, 6), (7, 8)):
        for c in fwd[index]:
            c.wait_recv()
        prepare(slot)
    for c in phase2:
        c.wait_recv()
    phase3 = [
        pltpu.make_async_remote_copy(mz_ref, mx_ref.at[xi], s3.at[d - 1], r3.at[d - 1],
                                     device_id=xpeer(d), device_id_type=MESH)
        for d in range(1, 8)
    ]
    for c in phase3:
        c.start()
    mx_ref[xi] = mz_ref[...]

    lane128 = lax.broadcasted_iota(jnp.int32, (128, 128), 1)

    def pairs(t):
        tm = tm_ref[t]
        accs, acc2 = None, None
        for k in range(8):
            i0, i1 = lists_ref[2 * k, t], lists_ref[2 * k + 1, t]
            f = jnp.concatenate([fb_ref[i0], fb_ref[i1]], axis=1)
            d = jnp.dot(tm, f, preferred_element_type=jnp.float32)
            r = lax.rsqrt(d)
            w = r * r * r
            if k in MX:
                p = jnp.concatenate([pb_ref[i0], pb_ref[i1]], axis=1)
                hi = w.astype(jnp.bfloat16)
                lo = (w - hi.astype(jnp.float32)).astype(jnp.bfloat16)
                y = lax.dot_general(hi, p, DN, preferred_element_type=jnp.float32)
                acc2 = y if acc2 is None else acc2 + y
                acc2 = acc2 + lax.dot_general(lo, p, DN, preferred_element_type=jnp.float32)
                continue
            for u, ii in enumerate((i0, i1)):
                wu = w[:, u * 128:(u + 1) * 128]
                g = [p_ref[pl.ds(ii * 8 + cc, 1), :] * wu for cc in range(4)]
                accs = g if accs is None else [x + y for x, y in zip(accs, g)]
        red2_ref[t] = acc2
        rr = [jnp.sum(x, axis=1, keepdims=True) for x in accs]
        red_ref[t] = jnp.where(lane128 == 0, rr[0], jnp.where(lane128 == 1, rr[1], jnp.where(lane128 == 2, rr[2], rr[3])))

    def reduce(t):
        v = v_ref[pl.ds((256 + t) * 8, 8), :]
        r2 = jnp.transpose(red2_ref[t])
        red = jnp.transpose(red_ref[t])[0:4] + (r2[0:4] + r2[4:8] + r2[8:12])
        for c in range(3):
            near_ref[c, pl.ds(t, 1), :] = red[c + 1:c + 2] - v[c:c + 1, :] * red[0:1]

    def slots(i, c):
        for u in range(UN):
            pairs(i * UN + u)
        for u in range(UN):
            reduce(jnp.maximum(i - 1, 0) * UN + u)
        return c

    lax.fori_loop(0, 32 // UN, slots, 0)
    for u in range(UN):
        reduce(32 - UN + u)

    for c in phase3:
        c.wait_recv()
    mt = jnp.transpose(mx_ref[...].reshape(64, 128))[:16, :]
    for g in range(32):
        mb_ref[pl.ds(g * 16, 16), :] = jnp.broadcast_to(mt[:, 2 * g:2 * g + 1] + mt[:, 2 * g + 1:2 * g + 2], (16, 128))

    def far(s, c):
        x, dy, dz = offsets(s)
        by, bz, ax = [None] * 8, [None] * 2, None
        for g in range(32):
            dx = (2.0 * g + 1.0 - fgx) - x
            total = None
            for j in range(8):
                w = [q_ref[s, g * 16 + j * 2 + h] * mb_ref[pl.ds(g * 16 + j * 2 + h, 1), :] for h in range(2)]
                bz = [w[h] if bz[h] is None else bz[h] + w[h] for h in range(2)]
                both = w[0] + w[1]
                by[j] = both if by[j] is None else by[j] + both
                total = both if total is None else total + both
            ax = total * dx if ax is None else ax + total * dx
        ay = by[0] * dy[0]
        for j in range(1, 8):
            ay = ay + by[j] * dy[j]
        az = bz[0] * dz[0] + bz[1] * dz[1]
        active = row8 + s * 8 < count_ref[0, 0]
        for k, val in enumerate((ax, ay, az)):
            at = pl.ds(pl.multiple_of(s * 8, 8), 8)
            out_ref[k, at, :] = jnp.where(active, near_ref[k, at, :] + val, 0.0)
        return c

    lax.fori_loop(0, 4, far, 0)
    for c in phase1 + phase2 + phase3 + toxp + toxm + toyp + toym + fwd[4] + fwd[5] + fwd[6] + fwd[7]:
        c.wait_send()


def forces(lists, count, ids, blk):
    dma = pltpu.SemaphoreType.DMA
    return pl.pallas_call(
        force_kernel,
        out_shape=jax.ShapeDtypeStruct((3, 32, 128), jnp.float32),
        in_specs=[pl.BlockSpec(memory_space=pltpu.SMEM)] * 2 + [pl.BlockSpec(memory_space=pltpu.VMEM),
                  pl.BlockSpec(memory_space=pl.ANY)],
        out_specs=pl.BlockSpec(memory_space=pltpu.VMEM),
        scratch_shapes=[
            pltpu.VMEM((8, 8, 1, 128), jnp.float32), pltpu.VMEM((3, 32, 128), jnp.float32),
            pltpu.VMEM((4, 512, 8, 128), jnp.float32), pltpu.VMEM((512, 128), jnp.float32),
            pltpu.VMEM((2304, 128), jnp.float32), pltpu.VMEM((4608, 128), jnp.float32),
            pltpu.VMEM((4608, 128), jnp.float32), pltpu.VMEM((576, 32, 128), jnp.bfloat16),
            pltpu.VMEM((576, 16, 128), jnp.bfloat16), pltpu.VMEM((32, 128, 32), jnp.bfloat16),
            pltpu.VMEM((32, 128, 128), jnp.float32), pltpu.VMEM((32, 128, 16), jnp.float32),
            pltpu.VMEM((1, 128), jnp.float32), pltpu.VMEM((15, 1, 128), jnp.float32),
            pltpu.VMEM((1, 128), jnp.float32), pltpu.VMEM((8, 1, 128), jnp.float32),
            dma((8 * NCH,)), dma((8 * NCH,)), dma((15,)), dma((15,)), dma((7,)), dma((7,)), dma((7,)), dma((7,)), dma,
        ],
        compiler_params=pltpu.CompilerParams(collective_id=0, has_side_effects=True),
        name="forces",
    )(lists, count, ids, blk)


def body(blocks, active_counts, pair_lists, cell_ids):
    out = forces(pair_lists[0, 0].T, active_counts, cell_ids[0], blocks.reshape(256, 128))
    return out.transpose(1, 0, 2)[None, None]


def solution(mesh):
    in_specs = (P("gx", "gy", None, None, None), P("gx", "gy"), P("gx", "gy", None, None), P("gx", "gy", None))
    return jax.shard_map(body, mesh=mesh, in_specs=in_specs, out_specs=P("gx", "gy", None, None, None),
                         check_vma=False)
```

```python
import jax
import jax.numpy as jnp
from jax import lax
from jax.experimental import pallas as pl
from jax.experimental.pallas import tpu as pltpu
from jax.sharding import PartitionSpec as P

MESH = pl.DeviceIdType.MESH
EPS2 = 0.05 * 0.05
NCH = 4
UN = 4
MX = (0, 2, 4, 6)
DN = (((1,), (1,)), ((), ()))


def split3(v):
    h = v.astype(jnp.bfloat16).astype(jnp.float32)
    r = v - h
    m = r.astype(jnp.bfloat16).astype(jnp.float32)
    return h, m, r - m


def force_kernel(lists_ref, count_ref, ids_ref, blk_ref, out_ref, mx_ref, near_ref, q_ref, mb_ref, tab_ref, v_ref, p_ref, fb_ref, pb_ref, tm_ref, red_ref,
                red2_ref, row1_ref, got1_ref, row2_ref, mz_ref, hs_sem, hr_sem, s1, r1, s2, r2, s3, r3, loc_sem):
    nx, ny = 64, 16
    gx, gy = lax.axis_index("gx"), lax.axis_index("gy")
    xi, zi = gx // 8, gx % 8
    xp, xm = lax.rem(gx + 1, nx), lax.rem(gx + nx - 1, nx)
    yp, ym = lax.rem(gy + 1, ny), lax.rem(gy + ny - 1, ny)

    def ypeer(d):
        return (gx, lax.rem(gy + d, ny))

    def zpeer(d):
        return (xi * 8 + lax.rem(zi + d, 8), gy)

    def xpeer(b):
        return ((xi + b - 2 * b * ((xi // b) % 2)) * 8 + zi, gy)

    barrier = pltpu.get_barrier_semaphore()
    for d in range(1, ny):
        pl.semaphore_signal(barrier, inc=1, device_id=ypeer(d), device_id_type=MESH)
    for d in range(1, 8):
        pl.semaphore_signal(barrier, inc=1, device_id=zpeer(d), device_id_type=MESH)
    for b in (1, 2, 4):
        pl.semaphore_signal(barrier, inc=1, device_id=xpeer(b), device_id_type=MESH)
    pl.semaphore_signal(barrier, inc=1, device_id=(xp, gy), device_id_type=MESH)
    pl.semaphore_signal(barrier, inc=1, device_id=(xm, gy), device_id_type=MESH)

    own = pltpu.make_async_copy(blk_ref, tab_ref.at[pl.ds(1024, 256)], loc_sem)
    own.start()

    pl.semaphore_wait(barrier, 27)

    size = 256 // NCH

    def halo(index, ch, source, slot, device):
        src = blk_ref.at[pl.ds(ch * size, size)] if source is None else tab_ref.at[pl.ds(source * 256 + ch * size, size)]
        k = index * NCH + ch
        return pltpu.make_async_remote_copy(src, tab_ref.at[pl.ds(slot * 256 + ch * size, size)], hs_sem.at[k],
                                            hr_sem.at[k], device_id=device, device_id_type=MESH)

    toxp = [halo(0, ch, None, 1, (xp, gy)) for ch in range(NCH)]
    toxm = [halo(1, ch, None, 7, (xm, gy)) for ch in range(NCH)]
    toyp = [halo(2, ch, None, 3, (gx, yp)) for ch in range(NCH)]
    toym = [halo(3, ch, None, 5, (gx, ym)) for ch in range(NCH)]
    fwd = {4: [], 5: [], 6: [], 7: []}
    for ch in range(NCH):
        for c in (toxp, toxm, toyp, toym):
            c[ch].start()

    own.wait()

    m = tab_ref[pl.ds(1024 + 3, 64, stride=4), :]
    ids = jnp.broadcast_to(ids_ref[...] % 2, (64, 64)).astype(jnp.float32)
    eye = lax.broadcasted_iota(jnp.int32, (64, 64), 0) == lax.broadcasted_iota(jnp.int32, (64, 64), 1)
    half = jnp.sum(jnp.where(eye, ids, 0.0), axis=1, keepdims=True)
    upper = jnp.sum(jnp.sum(jnp.where(half > 0.5, m, 0.0), axis=0, keepdims=True), axis=1, keepdims=True)
    lower = jnp.sum(jnp.sum(jnp.where(half > 0.5, 0.0, m), axis=0, keepdims=True), axis=1, keepdims=True)
    lane = lax.broadcasted_iota(jnp.int32, (1, 128), 1)
    at = (gy // 2) * 2
    row = jnp.where(lane == at, lower, jnp.where(lane == at + 1, upper, 0.0))
    row1_ref[...] = row

    phase1 = [
        pltpu.make_async_remote_copy(row1_ref, got1_ref.at[d - 1], s1.at[d - 1], r1.at[d - 1],
                                     device_id=ypeer(d), device_id_type=MESH)
        for d in range(1, ny)
    ]
    for c in phase1:
        c.start()

    low = lax.broadcasted_iota(jnp.int32, (8, 128), 0) < 4
    ones = jnp.ones((8, 128), jnp.float32)

    def prepare(q):
        a, b = q // 3 - 1, q % 3 - 1
        x = tab_ref[pl.ds(q * 256, 64, stride=4), :] + (a - 0.5)
        y = tab_ref[pl.ds(q * 256 + 1, 64, stride=4), :] + (b - 0.5)
        z = tab_ref[pl.ds(q * 256 + 2, 64, stride=4), :] - 0.5
        m = tab_ref[pl.ds(q * 256 + 3, 64, stride=4), :]
        s = x * x + y * y + z * z
        for k, val in enumerate((x, y, z, s, x, y, z, s)):
            v_ref[pl.ds(q * 512 + k, 64, stride=8), :] = val
        for k, val in enumerate((m, m * x, m * y, m * z) * 2):
            p_ref[pl.ds(q * 512 + k, 64, stride=8), :] = val

        def step(i, c):
            for u in range(4):
                j = q * 64 + i * 4 + u
                h, m, l = split3(v_ref[pl.ds(j * 8, 8), :])
                f = jnp.concatenate([jnp.where(low, h, m), jnp.where(low, l, h), jnp.where(low, m, h), ones], axis=0)
                fb_ref[j] = f.astype(jnp.bfloat16)
                h, m, l = split3(p_ref[pl.ds(j * 8, 8), :])
                pb_ref[j] = jnp.concatenate([jnp.where(low, h, m), l], axis=0).astype(jnp.bfloat16)
            return c

        lax.fori_loop(0, 16, step, 0)

    row8 = lax.broadcasted_iota(jnp.int32, (8, 128), 0)
    ws = (row8 & 3) == 3

    def targets(i, c):
        for u in range(4):
            t = i * 4 + u
            v = v_ref[pl.ds((256 + t) * 8, 8), :]
            h, m, l = split3(-2.0 * v)
            h = jnp.where(ws, 1.0, h)
            m = jnp.where(ws, 0.0, m)
            l = jnp.where(ws, 0.0, l)
            qh, qm, ql = split3(v[3:4, :] + EPS2)
            qg = jnp.where(row8 == 0, qh, jnp.where(row8 == 1, qm, jnp.where(row8 == 2, ql, 0.0)))
            tt = jnp.concatenate([h, jnp.where(low, h, m), jnp.where(low, m, l), qg], axis=0)
            tm_ref[t] = jnp.transpose(tt).astype(jnp.bfloat16)
        return c

    def forward(ch):
        for index, arrived, source, slot, device in ((4, toxp, 1, 0, (gx, yp)), (6, None, 1, 2, (gx, ym)),
                                                     (5, toxm, 7, 6, (gx, yp)), (7, None, 7, 8, (gx, ym))):
            if arrived is not None:
                arrived[ch].wait_recv()
            c = halo(index, ch, source, slot, device)
            c.start()
            fwd[index].append(c)

    fgx, fgy = gx.astype(jnp.float32), gy.astype(jnp.float32)

    def offsets(s):
        x = tab_ref[pl.ds(1024 + s * 32, 8, stride=4), :]
        y = tab_ref[pl.ds(1024 + s * 32 + 1, 8, stride=4), :]
        z = tab_ref[pl.ds(1024 + s * 32 + 2, 8, stride=4), :]
        return x, [(2.0 * j + 1.0 - fgy) - y for j in range(8)], [0.25 - z, 0.75 - z]

    def weights(s):
        x, dy, dz = offsets(s)
        zz = [d * d + 1.0 for d in dz]
        yy = [d * d for d in dy]
        base = [yy[j] + zz[h] for j in range(8) for h in range(2)]

        def step(i, c):
            for u in range(4):
                g = i * 4 + u
                dx = (2.0 * g.astype(jnp.float32) + 1.0 - fgx) - x
                xx = dx * dx
                for k in range(16):
                    r = lax.rsqrt(base[k] + xx)
                    q_ref[s, g * 16 + k] = r * r * r
            return c

        lax.fori_loop(0, 8, step, 0)

    prepare(4)
    for ch in range(NCH):
        forward(ch)
        weights(ch)
    lax.fori_loop(0, 8, targets, 0)
    red_ref[0:UN] = jnp.zeros((UN, 128, 128), jnp.float32)
    red2_ref[0:UN] = jnp.zeros((UN, 128, 16), jnp.float32)
    for c in phase1:
        c.wait_recv()
    total = row
    for d in range(1, ny):
        total = total + got1_ref[d - 1]
    row2_ref[...] = total
    mz_ref[zi] = total
    phase2 = [
        pltpu.make_async_remote_copy(row2_ref, mz_ref.at[zi], s2.at[d - 1], r2.at[d - 1],
                                     device_id=zpeer(d), device_id_type=MESH)
        for d in range(1, 8)
    ]
    for c in phase2:
        c.start()
    prepare(1)
    prepare(7)
    for c in toyp:
        c.wait_recv()
    prepare(3)
    for c in toym:
        c.wait_recv()
    prepare(5)
    for index, slot in ((4, 0), (6, 2), (5, 6), (7, 8)):
        for c in fwd[index]:
            c.wait_recv()
        prepare(slot)
    for c in phase2:
        c.wait_recv()
    mx_ref[xi] = mz_ref[...]

    def double(k):
        b = 1 << k
        part = mx_ref.at[pl.ds((xi // b) * b, b)]
        return pltpu.make_async_remote_copy(part, part, s3.at[k], r3.at[k], device_id=xpeer(b), device_id_type=MESH)

    first = pltpu.make_async_remote_copy(mz_ref, mx_ref.at[xi], s3.at[0], r3.at[0], device_id=xpeer(1),
                                         device_id_type=MESH)
    phase3 = [first, double(1), double(2)]
    phase3[0].start()

    lane128 = lax.broadcasted_iota(jnp.int32, (128, 128), 1)

    def pairs(t):
        tm = tm_ref[t]
        accs, acc2 = None, None
        for k in range(8):
            i0, i1 = lists_ref[2 * k, t], lists_ref[2 * k + 1, t]
            f = jnp.concatenate([fb_ref[i0], fb_ref[i1]], axis=1)
            d = jnp.dot(tm, f, preferred_element_type=jnp.float32)
            r = lax.rsqrt(d)
            w = r * r * r
            if k in MX:
                p = jnp.concatenate([pb_ref[i0], pb_ref[i1]], axis=1)
                hi = w.astype(jnp.bfloat16)
                lo = (w - hi.astype(jnp.float32)).astype(jnp.bfloat16)
                y = lax.dot_general(hi, p, DN, preferred_element_type=jnp.float32)
                acc2 = y if acc2 is None else acc2 + y
                acc2 = acc2 + lax.dot_general(lo, p, DN, preferred_element_type=jnp.float32)
                continue
            for u, ii in enumerate((i0, i1)):
                wu = w[:, u * 128:(u + 1) * 128]
                g = [p_ref[pl.ds(ii * 8 + cc, 1), :] * wu for cc in range(4)]
                accs = g if accs is None else [x + y for x, y in zip(accs, g)]
        red2_ref[t] = acc2
        rr = [jnp.sum(x, axis=1, keepdims=True) for x in accs]
        red_ref[t] = jnp.where(lane128 == 0, rr[0], jnp.where(lane128 == 1, rr[1], jnp.where(lane128 == 2, rr[2], rr[3])))

    def reduce(t):
        v = v_ref[pl.ds((256 + t) * 8, 8), :]
        r2 = jnp.transpose(red2_ref[t])
        red = jnp.transpose(red_ref[t])[0:4] + (r2[0:4] + r2[4:8] + r2[8:12])
        for c in range(3):
            near_ref[c, pl.ds(t, 1), :] = red[c + 1:c + 2] - v[c:c + 1, :] * red[0:1]

    def slots(i, c):
        for u in range(UN):
            pairs(i * UN + u)
        for u in range(UN):
            reduce(jnp.maximum(i - 1, 0) * UN + u)
        return c

    steps = 32 // UN
    cuts = (0, steps // 4, 5 * steps // 8, steps)
    for k in range(3):
        lax.fori_loop(cuts[k], cuts[k + 1], slots, 0)
        phase3[k].wait_recv()
        if k < 2:
            phase3[k + 1].start()
    for u in range(UN):
        reduce(32 - UN + u)

    mt = jnp.transpose(mx_ref[...].reshape(64, 128))[:16, :]
    for g in range(32):
        mb_ref[pl.ds(g * 16, 16), :] = jnp.broadcast_to(mt[:, 2 * g:2 * g + 1] + mt[:, 2 * g + 1:2 * g + 2], (16, 128))

    def far(s, c):
        x, dy, dz = offsets(s)
        by, bz, ax = [None] * 8, [None] * 2, None
        for g in range(32):
            dx = (2.0 * g + 1.0 - fgx) - x
            total = None
            for j in range(8):
                w = [q_ref[s, g * 16 + j * 2 + h] * mb_ref[pl.ds(g * 16 + j * 2 + h, 1), :] for h in range(2)]
                bz = [w[h] if bz[h] is None else bz[h] + w[h] for h in range(2)]
                both = w[0] + w[1]
                by[j] = both if by[j] is None else by[j] + both
                total = both if total is None else total + both
            ax = total * dx if ax is None else ax + total * dx
        ay = by[0] * dy[0]
        for j in range(1, 8):
            ay = ay + by[j] * dy[j]
        az = bz[0] * dz[0] + bz[1] * dz[1]
        active = row8 + s * 8 < count_ref[0, 0]
        for k, val in enumerate((ax, ay, az)):
            at = pl.ds(pl.multiple_of(s * 8, 8), 8)
            out_ref[k, at, :] = jnp.where(active, near_ref[k, at, :] + val, 0.0)
        return c

    lax.fori_loop(0, 4, far, 0)
    for c in phase1 + phase2 + phase3 + toxp + toxm + toyp + toym + fwd[4] + fwd[5] + fwd[6] + fwd[7]:
        c.wait_send()


def forces(lists, count, ids, blk):
    dma = pltpu.SemaphoreType.DMA
    return pl.pallas_call(
        force_kernel,
        out_shape=jax.ShapeDtypeStruct((3, 32, 128), jnp.float32),
        in_specs=[pl.BlockSpec(memory_space=pltpu.SMEM)] * 2 + [pl.BlockSpec(memory_space=pltpu.VMEM),
                  pl.BlockSpec(memory_space=pl.ANY)],
        out_specs=pl.BlockSpec(memory_space=pltpu.VMEM),
        scratch_shapes=[
            pltpu.VMEM((8, 8, 1, 128), jnp.float32), pltpu.VMEM((3, 32, 128), jnp.float32),
            pltpu.VMEM((4, 512, 8, 128), jnp.float32), pltpu.VMEM((512, 128), jnp.float32),
            pltpu.VMEM((2304, 128), jnp.float32), pltpu.VMEM((4608, 128), jnp.float32),
            pltpu.VMEM((4608, 128), jnp.float32), pltpu.VMEM((576, 32, 128), jnp.bfloat16),
            pltpu.VMEM((576, 16, 128), jnp.bfloat16), pltpu.VMEM((32, 128, 32), jnp.bfloat16),
            pltpu.VMEM((32, 128, 128), jnp.float32), pltpu.VMEM((32, 128, 16), jnp.float32),
            pltpu.VMEM((1, 128), jnp.float32), pltpu.VMEM((15, 1, 128), jnp.float32),
            pltpu.VMEM((1, 128), jnp.float32), pltpu.VMEM((8, 1, 128), jnp.float32),
            dma((8 * NCH,)), dma((8 * NCH,)), dma((15,)), dma((15,)), dma((7,)), dma((7,)), dma((3,)), dma((3,)), dma,
        ],
        compiler_params=pltpu.CompilerParams(collective_id=0, has_side_effects=True),
        name="forces",
    )(lists, count, ids, blk)


def body(blocks, active_counts, pair_lists, cell_ids):
    out = forces(pair_lists[0, 0].T, active_counts, cell_ids[0], blocks.reshape(256, 128))
    return out.transpose(1, 0, 2)[None, None]


def solution(mesh):
    in_specs = (P("gx", "gy", None, None, None), P("gx", "gy"), P("gx", "gy", None, None), P("gx", "gy", None))
    return jax.shard_map(body, mesh=mesh, in_specs=in_specs, out_specs=P("gx", "gy", None, None, None),
                         check_vma=False)
```
